256 devices in a mesh: tp: 8 (over x, z_lo), wide: 32 (over y, z_hi, core).
Axes of the slice: x: 4, y: 4, z: 8 (z_hi: 4, z_lo: 2; z = z_hi * 2 + z_lo), core: 2. Of those that a mesh axis runs over, the one named last changes fastest.
Arguments:
- token_keys: bfloat16 [4096, 28672], P('tp', 'wide'), may hold values from -6 to 6
- resid_grad: bfloat16 [4096, 8192], P('wide', 'tp'), may hold values from -6 to 6
- kv_grad: bfloat16 [4096, 2048], P('wide', 'tp'), may hold values from -6 to 6
- kv_weight: bfloat16 [8192, 2048], P('wide', 'tp'), may hold values from -0.125 to 0.125
- editor_in: bfloat16 [8192, 1920], P('tp'), may hold values from -0.0625 to 0.0625
- editor_bias: float32 [1920], replicated, may hold values from -3 to 3
- editor_gain: float32 [8192], P('tp'), may hold values from 0.5 to 1.5
- editor_out: bfloat16 [1920, 8192], P(None, 'tp'), may hold values from -0.125 to 0.125
- prompt_len: int32 [64], replicated, may hold values from 1 to 63
Outputs:
- weight_update: bfloat16 [28672, 8192], P('wide', 'tp')
The draws below stay inside these ranges and needn't reach their ends.
All inputs are finite; a program needn't handle non-finite values.
Results may differ from the reference program's by a relative error of at most 0.0055.
Values may be sent and summed in bfloat16 or wider, within the bound.
No kernel may reach another device: no remote copies, remote signals or barrier semaphores. Data moves between devices by JAX's collectives and lax.ppermute only.
A program may use at most 128 MiB of HBM per device.

```python
import jax
import jax.numpy as jnp
from jax import lax

D = 8192
FF = 28672
KV = 2048
RANK = 1920
LEN = 64
TOKENS = 4096
EXAMPLES = 64


def with_ends(entries, key, smallest, largest):
    longest = entries.shape.index(max(entries.shape))
    spots = []
    for shift in (0, 1):
        where = [jax.random.randint(jax.random.fold_in(key, axis), (), 0, length) for axis, length in enumerate(entries.shape)]
        where[longest] = (where[longest] + shift) % entries.shape[longest]
        spots.append(tuple(where))
    return entries.at[spots[0]].set(smallest).at[spots[1]].set(largest)


def level_of(key, dims, pieces, low, largest):
    def one(axis_at, blocks):
        draws = jax.random.uniform(jax.random.fold_in(jax.random.fold_in(key, 6), axis_at), (blocks,), jnp.float32, low / len(pieces), largest / len(pieces))
        return jnp.repeat(jnp.exp(draws), dims[axis_at] // blocks).reshape((-1,) + (1,) * (len(dims) - axis_at - 1))

    gain = one(*pieces[0])
    for cut in pieces[1:]:
        gain = gain * one(*cut)
    return gain


def noise(key, dims, spread, limit, split=(), held_as=jnp.bfloat16):
    factor_of = level_of(key, dims, split, -0.22, 0.18) if split else 1.0
    result = jax.random.normal(key, dims, jnp.float32) * spread * factor_of
    return jnp.minimum(jnp.maximum(result, -limit), limit).astype(held_as)


def setup_inputs(seed: int = 0) -> dict:
    key_of = jax.random.split(jax.random.key(seed), 10)
    token_keys = noise(key_of[0], (TOKENS, FF), 1.0, 6.0, ((0, 8), (1, 32)))
    resid_grad = noise(key_of[1], (TOKENS, D), 1.0, 6.0, ((0, 32), (1, 8)))
    kv_grad = noise(key_of[2], (TOKENS, KV), 1.0, 6.0, ((0, 32), (1, 8)))
    kv_weight = noise(key_of[3], (D, KV), KV ** -0.5, 0.125, ((0, 32), (1, 8)))
    editor_in = noise(key_of[4], (D, RANK), D ** -0.5, 0.0625, ((0, 8),))
    editor_bias = noise(key_of[5], (RANK,), 0.5, 3.0, (), jnp.float32)
    editor_gain = jnp.clip(1.0 + 0.1 * jax.random.normal(key_of[6], (D,), jnp.float32), 0.5, 1.5)
    editor_out = noise(key_of[7], (RANK, D), RANK ** -0.5, 0.125, ((1, 8),))
    prompt_len = with_ends(jax.random.randint(key_of[8], (EXAMPLES,), 1, LEN), jax.random.fold_in(key_of[8], 1), 1, LEN - 1).astype(jnp.int32)
    return {"token_keys": token_keys, "resid_grad": resid_grad, "kv_grad": kv_grad, "kv_weight": kv_weight, "editor_in": editor_in, "editor_bias": editor_bias, "editor_gain": editor_gain, "editor_out": editor_out, "prompt_len": prompt_len}


def reference(token_keys, resid_grad, kv_grad, kv_weight, editor_in, editor_bias, editor_gain, editor_out, prompt_len):
    kv_term = lax.dot_general(kv_grad, kv_weight, (((1,), (1,)), ((), ())), preferred_element_type=jnp.float32)
    gradient = resid_grad.astype(jnp.float32) + kv_term
    inv_rms = lax.rsqrt(lax.optimization_barrier(jnp.mean(gradient * gradient, axis=1, keepdims=True)) + 1e-06)
    scaled = (gradient * editor_gain.astype(jnp.float32)).astype(jnp.bfloat16)
    projected = jnp.dot(scaled, editor_in, preferred_element_type=jnp.float32)
    hidden = jnp.maximum(projected * inv_rms + editor_bias.astype(jnp.float32), 0.0).astype(jnp.bfloat16)
    starts = jnp.repeat(prompt_len.astype(jnp.int32), LEN, total_repeat_length=TOKENS)
    position = jnp.arange(TOKENS, dtype=jnp.int32) % LEN
    keep_mask = (position >= starts).astype(jnp.float32)
    edited = ((gradient + jnp.dot(hidden, editor_out, preferred_element_type=jnp.float32)) * keep_mask[:, None]).astype(jnp.bfloat16)
    edit_count = jnp.sum(LEN - prompt_len).astype(jnp.float32)
    summed = lax.dot_general(token_keys, edited, (((0,), (0,)), ((), ())), preferred_element_type=jnp.float32)
    return (summed * lax.rsqrt(edit_count)).astype(jnp.bfloat16)
```

```python
import jax
import jax.numpy as jnp
from jax import lax
from jax.experimental import pallas as pl
from jax.experimental.pallas import tpu as pltpu
from jax.sharding import PartitionSpec as P


LEN = 64
EPSILON = 1e-06
BF = jnp.bfloat16
F32 = jnp.float32


def tp_move(dx, dz):
    return [(2 * ((x + dx) % 4) + (z + dz) % 2, 2 * x + z) for x in range(4) for z in range(2)]


def wide_move(dy, dz, dc):
    return [
        (8 * ((y + dy) % 4) + 2 * ((z + dz) % 4) + (c + dc) % 2, 8 * y + 2 * z + c)
        for y in range(4)
        for z in range(4)
        for c in range(2)
    ]


def from_tp(value, dx, dz):
    return lax.ppermute(value, "tp", tp_move(dx, dz))


def from_wide(value, dy, dz, dc=0):
    return lax.ppermute(value, "wide", wide_move(dy, dz, dc))


def weight_move():
    moves = []
    for x in range(4):
        for zl in range(2):
            for w in range(32):
                y, high, low, c = w // 8, (w // 4) % 2, (w // 2) % 2, w % 2
                dest_y = (2 * y + 2 - x) % 4
                dest_z = (2 * low + zl + 3 + 2 * high) % 4
                moves.append(((2 * x + zl) * 32 + w, (2 * y + high) * 32 + 8 * dest_y + 2 * dest_z + c))
    return moves


def call(kernel, out_shape, n_in, scalars=1, scratch=(), in_specs=None, out_specs=None, limit=16, **kw):
    smem = pl.BlockSpec(memory_space=pltpu.SMEM)
    vmem = pl.BlockSpec(memory_space=pltpu.VMEM)
    if in_specs is None:
        in_specs = [vmem] * n_in
    if out_specs is None:
        out_specs = jax.tree.map(lambda _: vmem, out_shape)
    return pl.pallas_call(
        kernel,
        out_shape=out_shape,
        in_specs=[smem] * scalars + in_specs,
        out_specs=out_specs,
        scratch_shapes=list(scratch),
        compiler_params=pltpu.CompilerParams(vmem_limit_bytes=limit * 1024 * 1024),
        **kw,
    )


def dot_nt(a, b):
    return lax.dot_general(a, b, (((1,), (1,)), ((), ())), preferred_element_type=F32)


def dot_nn(a, b):
    return lax.dot_general(a, b, (((1,), (0,)), ((), ())), preferred_element_type=F32)


def kv_kernel(places):
    def body(pos, grads, grads_other, staged, *refs):
        weights, (mine, other, right) = refs[:-3], refs[-3:]
        x, zl, y, zh = pos[0], pos[1], pos[2], pos[3]
        for ref, spots in zip(weights, places):
            for i, (dy, dz) in enumerate(spots):
                yy = (y + dy) % 4
                zz = (zh + dz) % 4
                xx = (2 * x + 2 - yy + 4) % 4
                s = (zz + 1 + 2 * zl) % 4
                slot = ((xx - x + 4) % 4) * 2 + (s % 2 + zl) % 2
                right[s // 2, slot] = ref[i * 256 : (i + 1) * 256, :] if len(ref.shape) == 2 else ref[i]
        for b in range(2):
            cols = slice(b * 256, (b + 1) * 256)
            total = jnp.zeros((256, 256), F32)
            for slot in range(8):
                rows = slice(slot * 128, (slot + 1) * 128)
                left = jnp.concatenate([grads[rows, :], grads_other[rows, :]], axis=0)
                total = total + dot_nt(left, right[b, slot])
            mine[:, cols] = total[:128]
            other[:, cols] = total[128:]

    return body


def project_kernel(pos, mine, recv, resid, gain, editor_in, grad, payload, kv, scaled):
    c = pos[4]
    for b in range(2):
        part = slice(b * 256, (b + 1) * 256)
        kv[2 * b + c] = mine[:, part]
        kv[2 * b + 1 - c] = recv[:, part]
    squares = jnp.zeros((128, 1), F32)
    for h in range(4):
        cols = slice(h * 256, (h + 1) * 256)
        g = resid[:, cols].astype(F32) + kv[h]
        grad[:, cols] = g
        squares = squares + jnp.sum(g * g, axis=1, keepdims=True)
        scaled[:, cols] = (g * gain[:, cols]).astype(BF)

    payload[:, :1920] = dot_nn(scaled[...], editor_in[...]).astype(BF)

    high = squares.astype(BF)
    low = (squares - high.astype(F32)).astype(BF)
    lane = lax.broadcasted_iota(jnp.int32, (128, 128), 1)
    payload[:, 1920:] = jnp.where(lane < 64, high.astype(F32), low.astype(F32)).astype(BF)


def hidden_kernel(parts, bias, hidden):
    total = parts[0:16, :].astype(F32)
    for i in range(1, 8):
        total = total + parts[16 * i : 16 * (i + 1), :].astype(F32)
    squares = total[:, 1920:1921] + total[:, 2047:2048]
    inv_rms = lax.rsqrt(squares / 8192 + EPSILON)
    value = jnp.maximum(total[:, :1920] * inv_rms + bias[...], 0.0).astype(BF)
    for i in range(8):
        hidden[16 * i : 16 * (i + 1), :] = value


def edit_kernel(pos, prompt_len, hidden, editor_out, grad, edited):
    w = pos[5]
    row = lax.broadcasted_iota(jnp.int32, (128, 1), 0)
    start = jnp.where(row < LEN, prompt_len[2 * w], prompt_len[2 * w + 1])
    keep = ((row % LEN) >= start).astype(F32)
    value = grad[...] + dot_nn(hidden[...], editor_out[...])
    edited[...] = (value * keep).astype(BF)


def stage_kernel(*refs):
    n = (len(refs) - 1) // 2
    copies = [pltpu.make_async_copy(refs[i], refs[n + i], refs[-1]) for i in range(n)]
    for copy in copies:
        copy.start()
    for copy in copies:
        copy.wait()


def pieces_of(ref):
    return [ref] if len(ref.shape) == 2 else [ref.at[i] for i in range(ref.shape[0])]


def pack_kernel(*refs):
    out, sem = refs[-2:]
    copies = []
    row = 0
    for ref in refs[:-2]:
        for piece in pieces_of(ref):
            n = piece.shape[0]
            copies.append(pltpu.make_async_copy(piece, out.at[pl.ds(row, n), :], sem))
            row += n
    for copy in copies:
        copy.start()
    for copy in copies:
        copy.wait()


def turn_kernel(keys, turned):
    turned[...] = keys[...].T


def slots_zero(i):
    return i, 0


def slots_near(i):
    j = i % 3
    return j + j // 2, jnp.where(i < 3, 1, 3)


def slots_rest(i):
    return jnp.where(i < 4, i, 2), jnp.where(i < 4, 2, jnp.where(i < 5, 1, 3))


def update_kernel(n_own, n_swapped, slots, first, last):
    def body(pos, prompt_len, *refs):
        own = refs[:n_own]
        swapped = refs[n_own : n_own + n_swapped]
        rest = refs[n_own + n_swapped :]
        if first:
            keys = rest[:9]
            out, near_buf, rest_buf, left, edit_buf, edit_sem, key_sem, ahead_sem = rest[9:]
        else:
            acc, left, out, edit_buf, edit_sem = rest
        x, zl, y, zh, c = pos[0], pos[1], pos[2], pos[3], pos[4]

        def fetch(slot_of, n, buf, sem):
            @pl.loop(0, n)
            def _(i):
                dy, dz = slot_of(i)
                dx = (y + dy - x + 4) % 4
                zz = (zh + dz) % 4
                side = (zz // 2 + zl) % 2
                columns = pl.ds(pl.multiple_of((zz % 2) * 256, 256), 256)
                to = pl.ds(pl.multiple_of(i * 256, 256), 256)
                for k in range(4):
                    for z in range(2):

                        @pl.when((dx == k) & (side == z))
                        def _():
                            parts = ((keys[5], 0), (keys[8], 448)) if (k, z) == (2, 1) else ((keys[2 * k + z], 0),)
                            for part, row in parts:
                                rows = slice(row, row + part.shape[0])
                                pltpu.make_async_copy(part.at[:, columns], buf.at[rows, to], sem).start()

        copies = []
        for refs_of, core in ((own, c), (swapped, 1 - c)):
            at = 0
            for ref in refs_of:
                for whole in pieces_of(ref):
                    for k in range(whole.shape[0] // 128):
                        row = pl.multiple_of(slots[at] * 256 + core * 128, 128)
                        piece = whole.at[pl.ds(k * 128, 128), :]
                        copy = pltpu.make_async_copy(piece, edit_buf.at[pl.ds(row, 128), :], edit_sem)
                        copy.start()
                        copies.append(copy)
                        at += 1
        if first:
            fetch(slots_zero, 4, left, key_sem)
            fetch(slots_near, 6, near_buf, ahead_sem)
            fetch(slots_rest, 6, rest_buf, ahead_sem)
        for copy in copies:
            copy.wait()
        if last:
            count = lax.fori_loop(0, 64, lambda i, total: total + (LEN - prompt_len[i]), jnp.int32(0))
            scale = lax.rsqrt(jnp.full((1, 256), count.astype(F32)))
        if first:
            pltpu.make_async_copy(left, left, key_sem).wait()

        @pl.loop(0, 4)
        def _(j):
            cols = pl.ds(pl.multiple_of(j * 256, 256), 256)
            part = dot_nn(left[...], edit_buf[:, cols])
            if not first:
                part = part + acc[:, cols]
            out[:, cols] = (part * scale).astype(BF) if last else part

        if first:
            pltpu.make_async_copy(near_buf, near_buf, ahead_sem).wait()
            pltpu.make_async_copy(rest_buf, rest_buf, ahead_sem).wait()

    return body


def per_device(
    token_keys,
    resid_grad,
    kv_grad,
    kv_weight,
    editor_in,
    editor_bias,
    editor_gain,
    editor_out,
    prompt_len,
):
    t = lax.axis_index("tp")
    w = lax.axis_index("wide")
    x, zl = t // 2, t % 2
    y, zh, c = w // 8, (w // 2) % 4, w % 2
    pos = jnp.stack([x, zl, y, zh, c, w, t, t]).astype(jnp.int32)
    sds = jax.ShapeDtypeStruct

    k_own = call(turn_kernel, sds((896, 512), BF), 1, scalars=0)(token_keys)

    def swap(value):
        return from_wide(value, 0, 0, 1)

    w00 = lax.ppermute(kv_weight, ("tp", "wide"), weight_move())[None]
    g_z = from_tp(kv_grad, 0, 1)
    any_spec = pl.BlockSpec(memory_space=pl.ANY)
    vmem = pl.BlockSpec(memory_space=pltpu.VMEM)

    def pack(arrays):
        rows = sum(a.size for a in arrays) // arrays[0].shape[-1]
        return call(
            pack_kernel,
            sds((rows, arrays[0].shape[-1]), BF),
            0,
            scalars=0,
            in_specs=[any_spec] * len(arrays),
            scratch=[pltpu.SemaphoreType.DMA(())],
        )(*arrays)

    g0 = pack([kv_grad, g_z])
    g_all = pack([g0] + [from_tp(g0, dx, 0) for dx in (1, 2, 3)])
    g_other = swap(g_all)
    k_z = from_tp(k_own, 0, 1)
    k_x1 = from_tp(k_own, 1, 0)
    k_x3 = from_tp(k_own, 3, 0)
    k_x2 = from_tp(k_own, 2, 0)

    def spread(value, forward):
        z = {dz: from_wide(value, 0, dz) for dz in (1, 3)}
        if forward:
            near = {1: z[1][:, :64], 3: z[3][:, 64:]}
            far = [from_wide(near[dz], 0, dz) for dz in (1, 3)]
            z[2] = jnp.concatenate(far, axis=1)
        else:
            z[2] = from_wide(value, 0, 2)
        groups = []
        if forward:
            pair = jnp.concatenate([z[1], z[3]], axis=0)
            sources = ((value, [0]), (pair, [1, 3]), (z[2], [2]))
        else:
            sources = ((value, [0]), (pack([z[1], z[3], z[2]]), [1, 3, 2]))
        for i, (array, spots) in enumerate(sources):
            arrays = [(array, [(0, dz, 0) for dz in spots])]
            moved = {}
            split = forward and i == 1
            for dy in (1, 3) if split else (1, 3, 2):
                moved[dy] = from_wide(array, dy, 0)
                arrays.append((moved[dy], [(dy, dz, 0) for dz in spots]))
            if split:
                for j, dy in enumerate((1, 3)):
                    piece = moved[dy][j : j + 1]
                    piece = from_wide(piece, dy, 0)
                    arrays.append((piece, [(2, spots[j], 0)]))
            groups.append(arrays)
        return groups

    ahead = (resid_grad, editor_gain.reshape(1, -1), editor_bias.reshape(1, -1), editor_in, editor_out)
    resid_s, gain_s, bias_s, in_s, out_s = call(
        stage_kernel,
        [sds(a.shape, a.dtype) for a in ahead],
        0,
        scalars=0,
        in_specs=[pl.BlockSpec(memory_space=pltpu.HBM)] * 5,
        scratch=[pltpu.SemaphoreType.DMA(())],
    )(*ahead)
    w_parts = sum(spread(w00, False), [])
    half = sds((128, 512), F32)
    mine, other = call(
        kv_kernel([[spot[:2] for spot in spots] for _, spots in w_parts]),
        (half, half),
        3 + len(w_parts),
        scratch=[pltpu.VMEM((2, 8, 256, 256), BF)],
    )(pos, g_all, g_other, gain_s, *[array for array, _ in w_parts])
    recv = swap(other)
    grad, payload = call(
        project_kernel,
        (sds((128, 1024), F32), sds((128, 2048), BF)),
        5,
        scratch=[pltpu.VMEM((4, 128, 256), F32), pltpu.VMEM((128, 1024), BF)],
    )(pos, mine, recv, resid_s, gain_s, in_s)
    parts = lax.all_to_all(payload, "tp", 0, 0, tiled=True)
    copies = call(hidden_kernel, sds((128, 1920), BF), 2, scalars=0)(parts, bias_s)
    hidden = lax.all_to_all(copies, "tp", 0, 0, tiled=True)
    edited = call(edit_kernel, sds((128, 1024), BF), 3, scalars=2)(pos, prompt_len, hidden, out_s, grad)

    edited, k_x2, k_z = lax.optimization_barrier((edited, k_x2, k_z))
    e_parts = spread(edited[None], True)
    k_zx1 = from_tp(k_z, 1, 0)
    k_zx3 = from_tp(k_z, 3, 0)
    top = from_tp(k_x2[:448], 0, 1)
    bottom = from_tp(k_z[448:], 2, 0)
    keys = [k_own, k_z, k_x1, k_zx1, k_x2, top, k_x3, k_zx3, bottom]

    by_dy = [{spots[0][0]: array for array, spots in group if len(spots) != 1 or i != 1} for i, group in enumerate(e_parts)]
    far = [array for array, spots in e_parts[1] if len(spots) == 1]
    dma = pltpu.SemaphoreType.DMA(())

    def update(i, own, swapped, slots, extra, extra_specs, out_shape, scratch):
        rows = 256 * len(slots)
        return call(
            update_kernel(len(own), len(swapped), slots, i == 0, i == 2),
            out_shape,
            0,
            scalars=2,
            in_specs=[any_spec] * (len(own) + len(swapped)) + extra_specs,
            scratch=[*scratch, pltpu.VMEM((rows, 1024), BF), dma] + ([dma, dma] if i == 0 else []),
            limit=20,
        )(pos, prompt_len, *own, *swapped, *extra)

    zero = [by_dy[0][dy] for dy in (0, 1, 3, 2)]
    near = [by_dy[1][dy] for dy in (0, 1, 3)]
    rest = [by_dy[2][dy] for dy in (0, 1, 3)] + far + [by_dy[2][2]]
    zero_swapped = [swap(pack(zero))]
    near_swapped = [swap(pack(near))]
    ahead = sds((896, 1536), BF)
    total, near_keys, rest_keys = update(
        0,
        zero,
        zero_swapped,
        [0, 1, 3, 2],
        keys,
        [any_spec] * 9,
        (sds((896, 1024), F32), ahead, ahead),
        [pltpu.VMEM((896, 1024), BF)],
    )
    rest_swapped = [swap(pack(rest[:5])), swap(rest[5])]
    near_slots = [0, 3, 1, 4, 2, 5]
    total = update(1, near, near_swapped, near_slots, (total, near_keys), [vmem] * 2, sds((896, 1024), F32), [])
    rest_slots = [0, 1, 3, 4, 5, 2]
    return update(2, rest, rest_swapped, rest_slots, (total, rest_keys), [vmem] * 2, sds((896, 1024), BF), [])


def solution(mesh):
    in_specs = (
        P("tp", "wide"),
        P("wide", "tp"),
        P("wide", "tp"),
        P("wide", "tp"),
        P("tp", None),
        P(),
        P("tp"),
        P(None, "tp"),
        P(),
    )
    out_specs = P("wide", "tp")
    return jax.shard_map(per_device, mesh=mesh, in_specs=in_specs, out_specs=out_specs, check_vma=False)
```
